32 devices in a mesh: windows: 2 (over x), tiles: 16 (over z, y, core).
Axes of the slice: x: 2, y: 2, z: 4, core: 2. Of those that a mesh axis runs over, the one named last changes fastest.
Arguments:
- data: bfloat16 [16, 2, 2048, 128], P('windows', None, 'tiles'), parts along dimension 0, may hold values from -6 to 6
- wavelet: float32 [8, 2], replicated, may hold values from -4 to 4
- panel_block: int32 [1], replicated, may hold values from 0 to 15
- tiles: bfloat16 [512, 2, 128, 128], P(('windows', 'tiles')), parts along dimension 0, may hold values from -0.25 to 0.25
- cover_rows: int32 [512], P(('windows', 'tiles')), parts along dimension 0, may hold values from 0 to 15, as said below
- cover_freqs: int32 [512], P(('windows', 'tiles')), parts along dimension 0, may hold values from 0 to 7
Outputs:
- residual: float32 [16, 2, 2048, 128], P('windows', None, 'tiles'), parts along dimension 0
- gradient: bfloat16 [512, 2, 128, 128], P(('windows', 'tiles')), parts along dimension 0
The draws below stay inside these ranges and needn't reach their ends.
There are 2 independent parts, one for each index of `windows`. The reference program is written for one: setup_inputs(seed, part) draws one part's arguments, and reference() takes and returns one part's arrays. A program takes and returns all parts, laid end to end along the dimension named above; an argument that names none is the same for every part. Nothing has to cross between parts.
Inputs may be any that keep to these rules, and one draw needn't show every extreme that they name: `cover_rows`: among the 16 entries of one column block no row block appears more than 2 times, exactly 12 distinct row blocks appear, one row block appears 2 times in every column block, and together with cover_freqs the entries of one column block name distinct (row block, frequency) pairs.
All inputs are finite; a program needn't handle non-finite values.
Results may differ from the reference program's by a relative error of at most 0.0053.
Values may be sent and summed in bfloat16 or wider, within the bound.
A program may use at most 128 MiB of HBM per device.

```python
import jax
import jax.numpy as jnp
from jax import lax

BLOCK = 128
PS = 128
FREQ = 8
SLOTS = 16
NR = 2048
TILES_ALL = 256
N_TILES = 16


def coverage_lists(key):
    hottest = jax.random.randint(jax.random.fold_in(key, 11), (), 0, N_TILES)
    column_keys = jax.random.split(jax.random.fold_in(key, 12), N_TILES)
    used = 3 * N_TILES // 4
    twice = N_TILES // 4

    def one_column(column_key):
        key_rank, key_start, key_second, key_order = jax.random.split(column_key, 4)
        blocks = jnp.arange(N_TILES, dtype=jnp.int32)
        ranking = jax.random.permutation(key_rank, N_TILES).astype(jnp.int32)
        ranking = jnp.where(blocks == N_TILES - 1, -1, ranking)
        ranking = jnp.where(blocks == hottest, -2, ranking)
        ordering = jnp.argsort(ranking, stable=True).astype(jnp.int32)
        rows = jnp.concatenate([ordering[:used], ordering[:twice]])
        offset = jax.random.randint(key_start, (), 0, FREQ)
        first_freqs = (offset + jnp.arange(used, dtype=jnp.int32)) % FREQ
        shifts = jax.random.randint(key_second, (twice,), 0, FREQ - 1)
        second_freqs = (first_freqs[:twice] + 1 + shifts) % FREQ
        freqs = jnp.concatenate([first_freqs, second_freqs])
        shuffle = jax.random.permutation(key_order, N_TILES)
        return (rows[shuffle], freqs[shuffle])
    rows, freqs = jax.vmap(one_column)(column_keys)
    return (rows.reshape(-1).astype(jnp.int32), freqs.reshape(-1).astype(jnp.int32))


def draw_cover_rows(key, part):
    return coverage_lists(key)[0]


def draw_cover_freqs(key, part):
    return coverage_lists(key)[1]


def block_levels(stream_key, extent, cuts, smallest, largest):
    factor_of, own = 1.0, jax.random.fold_in(stream_key, 6)
    for axis_at, blocks in cuts:
        steps = jnp.exp(jax.random.uniform(jax.random.fold_in(own, axis_at), (blocks,), jnp.float32, smallest / len(cuts), largest / len(cuts)))
        factor_of = factor_of * jnp.repeat(steps, extent[axis_at] // blocks).reshape([-1 if axis == axis_at else 1 for axis in range(len(extent))])
    return factor_of


def normal_values(key, dims, spread, limit, cuts=(), kind=jnp.bfloat16):
    result = spread * jax.random.normal(key, dims, jnp.float32)
    if cuts:
        result = result * block_levels(key, dims, cuts, -0.22, 0.18)
    return jnp.clip(result, -limit, limit).astype(kind)


def setup_inputs(seed: int = 0, part: int = 0) -> dict:
    seeds = jax.random.split(jax.random.key(seed), 7)
    part_keys = jax.random.split(jax.random.fold_in(seeds[6], part), 7)
    data = normal_values(part_keys[0], (FREQ, 2, NR, PS), 1.0, 6.0, ((2, 16),))
    wavelet = normal_values(seeds[1], (FREQ, 2), 1.0, 4.0, (), jnp.float32)
    panel_block = jax.random.randint(seeds[2], (1,), 0, N_TILES).astype(jnp.int32)
    tiles = normal_values(part_keys[3], (TILES_ALL, 2, BLOCK, BLOCK), (2 * BLOCK * N_TILES // FREQ) ** -0.5, 0.25, ((0, 16),))
    cover_rows = draw_cover_rows(jax.random.fold_in(jax.random.fold_in(seeds[6], part), 71), part)
    cover_freqs = draw_cover_freqs(jax.random.fold_in(jax.random.fold_in(seeds[6], part), 71), part)
    return dict(data=data, wavelet=wavelet, panel_block=panel_block, tiles=tiles, cover_rows=cover_rows, cover_freqs=cover_freqs)


def complex_product(left, right):
    left = left.astype(jnp.float32)
    right = right.astype(jnp.float32)

    def product(first, second):
        return jnp.einsum("sab,sbp->sap", first, second)

    real_part = product(left[:, 0], right[:, 0]) - product(left[:, 1], right[:, 1])
    imag_part = product(left[:, 0], right[:, 1]) + product(left[:, 1], right[:, 0])
    return jnp.stack([real_part, imag_part], axis=1)


def shot_gradient(rows_res, rows_src):
    rows_res = rows_res.astype(jnp.float32)
    rows_src = rows_src.astype(jnp.float32)
    scale = 1.0 / PS

    def outer(first, second):
        return jnp.einsum("kap,kbp->kab", first, second)

    real_part = -(outer(rows_res[:, 0], rows_src[:, 0]) + outer(rows_res[:, 1], rows_src[:, 1])) * scale
    imag_part = -(outer(rows_res[:, 1], rows_src[:, 0]) - outer(rows_res[:, 0], rows_src[:, 1])) * scale
    return jnp.stack([real_part, imag_part], axis=1).astype(jnp.bfloat16)


def reference(data, wavelet, panel_block, tiles, cover_rows, cover_freqs):
    row_ids = jnp.arange(BLOCK * N_TILES, dtype=jnp.int32)[:, None]
    col_ids = jnp.arange(PS, dtype=jnp.int32)[None, :]
    identity = (row_ids - panel_block[0] * BLOCK == col_ids).astype(jnp.float32)
    source_re = -data[:, 0].astype(jnp.float32) + wavelet[:, 0, None, None] * identity
    source_im = -data[:, 1].astype(jnp.float32) + wavelet[:, 1, None, None] * identity
    source = jnp.stack([source_re, source_im], axis=1).astype(jnp.bfloat16)
    source_cols = source.reshape(FREQ, 2, N_TILES, BLOCK, PS).transpose(2, 0, 1, 3, 4)
    tile_cols = tiles.reshape(N_TILES, SLOTS, 2, BLOCK, BLOCK)
    row_cols = cover_rows.reshape(N_TILES, SLOTS)
    freq_cols = cover_freqs.reshape(N_TILES, SLOTS)

    def forward(total, column):
        tile_set, rows, freqs, column_src = column
        parts = complex_product(tile_set, column_src[freqs]).astype(jnp.bfloat16)
        return total.at[freqs, rows].add(parts.astype(jnp.float32)), None

    start = jnp.zeros((FREQ, N_TILES, 2, BLOCK, PS), jnp.float32)
    total, _ = lax.scan(forward, start, (tile_cols, row_cols, freq_cols, source_cols))
    predicted = total.transpose(0, 2, 1, 3, 4).reshape(FREQ, 2, N_TILES * BLOCK, PS)
    residual = data.astype(jnp.float32) - predicted
    res_blocks = residual.astype(jnp.bfloat16).reshape(FREQ, 2, N_TILES, BLOCK, PS).transpose(0, 2, 1, 3, 4)

    def backward(carry, column):
        rows, freqs, column_src = column
        return carry, shot_gradient(res_blocks[freqs, rows], column_src[freqs])

    _, grads = lax.scan(backward, jnp.zeros((), jnp.float32), (row_cols, freq_cols, source_cols))
    return residual, grads.reshape(N_TILES * SLOTS, 2, BLOCK, BLOCK)
```

```python
import functools

import jax
import jax.numpy as jnp
from jax import lax
from jax.experimental import pallas as pl
from jax.experimental.pallas import tpu as pltpu
from jax.sharding import PartitionSpec as P

CAP = 2
FAR, NEAR = 0, 1
F32, BF16 = jnp.float32, jnp.bfloat16


def kernel(
    n, wav_ref, panel_ref, rows_ref, freqs_ref, data_ref, tiles_ref, res_ref, grad_ref,
    src, tag_send, tag_recv, send, recv, part_sum, far_send, far_recv, res_bf, back_recv,
    back, ret, s_tag, r_tag, s_fwd, r_fwd, s_far, r_far, s_mid, r_mid, s_ret, r_ret,
):
    nf, _, nb, ns = data_ref.shape
    slots = tiles_ref.shape[0]
    half = n // 2
    me = lax.axis_index("tiles")
    base = (me // half) * half
    local = lax.rem(me, half)
    mirror = lax.rem(me + half, n)

    def ahead(k):
        return base + lax.rem(local + k, half)

    def behind(k):
        return base + lax.rem(local + half - k, half)

    def remote(src_ref, dst_ref, s_sem, r_sem, device):
        return pltpu.make_async_remote_copy(
            src_ref=src_ref, dst_ref=dst_ref, send_sem=s_sem, recv_sem=r_sem,
            device_id={"tiles": device}, device_id_type=pl.DeviceIdType.MESH,
        )

    def tag_copy(k):
        return remote(tag_send.at[k], tag_recv.at[k], s_tag.at[k], r_tag.at[k], ahead(k))

    def fwd_copy(k, side, g):
        return remote(send.at[k, side, g], recv.at[k, side, g],
                      s_fwd.at[k, side, g], r_fwd.at[k, side, g], ahead(k))

    def far_copy(f, g):
        return remote(far_send.at[f, g], far_recv.at[f, g], s_far.at[f, g], r_far.at[f, g], mirror)

    def mid_copy(f, g):
        return remote(res_bf.at[f, g], back_recv.at[f, g], s_mid.at[f, g], r_mid.at[f, g], mirror)

    def ret_copy(k, side, g):
        return remote(back.at[k, side, g], ret.at[k, side, g],
                      s_ret.at[k, side, g], r_ret.at[k, side, g], behind(k))

    def loop(lo, hi, body):
        def step(i, carry):
            body(i)
            return carry
        lax.fori_loop(lo, hi, step, 0)

    barrier = pltpu.get_barrier_semaphore()

    def greet(k):
        pl.semaphore_signal(barrier, inc=1, device_id={"tiles": ahead(k)},
                            device_id_type=pl.DeviceIdType.MESH)
    loop(1, half, greet)
    pl.semaphore_signal(barrier, inc=1, device_id={"tiles": mirror},
                        device_id_type=pl.DeviceIdType.MESH)

    eye = lax.broadcasted_iota(jnp.int32, (nb, ns), 0) == lax.broadcasted_iota(jnp.int32, (nb, ns), 1)
    at_panel = jnp.where(me == panel_ref[0], 1.0, 0.0).astype(F32)

    def make_source(f):
        re = jnp.where(eye, at_panel * wav_ref[f, 0], 0.0) - data_ref[f, 0].astype(F32)
        im = jnp.where(eye, at_panel * wav_ref[f, 1], 0.0) - data_ref[f, 1].astype(F32)
        re, im = re.astype(BF16), im.astype(BF16)
        src[f, :nb, :ns] = re
        src[f, :nb, ns:] = im
        src[f, nb:, :ns] = -im
        src[f, nb:, ns:] = re
    loop(0, nf, make_source)

    def find(row):
        first = jnp.int32(-1)
        second = jnp.int32(-1)
        for t in reversed(range(slots)):
            hit = rows_ref[t] == row
            second = jnp.where(hit, first, second)
            first = jnp.where(hit, jnp.int32(t), first)
        return first, second

    def make_parts(k, side):
        row = ahead(k)
        if side == FAR:
            row = lax.rem(row + half, n)
        for c, t in enumerate(find(row)):
            at = jnp.maximum(t, 0)
            freq = freqs_ref[at]
            tag = jnp.where(t >= 0, freq, -1).astype(F32)
            tag_send[k, side * CAP + c : side * CAP + c + 1, :] = jnp.full((1, ns), tag, F32)
            left = jnp.concatenate([tiles_ref[at, 0], tiles_ref[at, 1]], axis=1)
            part = jnp.dot(left, src[freq], preferred_element_type=F32).astype(BF16)
            send[k, side, 0, c] = part[:, :ns]
            send[k, side, 1, c] = part[:, ns:]

    pl.semaphore_wait(barrier, half)

    def send_far(k):
        make_parts(k, FAR)
        fwd_copy(k, FAR, 0).start()
    loop(1, half, send_far)

    def send_far_rest(k):
        fwd_copy(k, FAR, 1).start()
    loop(1, half, send_far_rest)

    def send_near(k):
        make_parts(k, NEAR)
        tag_copy(k).start()
        fwd_copy(k, NEAR, 0).start()
        fwd_copy(k, NEAR, 1).start()
    loop(1, half, send_near)
    make_parts(0, FAR)
    make_parts(0, NEAR)

    def wait_tag(k):
        tag_copy(k).wait()
    loop(1, half, wait_tag)

    def gathered(side, f, g):
        want = f.astype(F32)

        def add(tags, parts, k, acc):
            for c in range(CAP):
                tag = tags[k, side * CAP + c : side * CAP + c + 1, :]
                acc = acc + jnp.where(tag == want, parts[k, side, g, c].astype(F32), 0.0)
            return acc
        acc = add(tag_send, send, 0, jnp.zeros((nb, ns), F32))
        return lax.fori_loop(1, half, functools.partial(add, tag_recv, recv), acc)

    def wait_fwd(side, g):
        def body(k):
            fwd_copy(k, side, g).wait()
        loop(1, half, body)

    for g in range(2):
        wait_fwd(FAR, g)

        def sum_far(f, g=g):
            far_send[f, g] = gathered(FAR, f, g).astype(BF16)
            far_copy(f, g).start()
        loop(0, nf, sum_far)
    for g in range(2):
        wait_fwd(NEAR, g)

        def sum_near(f, g=g):
            part_sum[f, g] = data_ref[f, g].astype(F32) - gathered(NEAR, f, g)
        loop(0, nf, sum_near)

    def give_back(side, g, rows):
        def pick(tags, k, out):
            for c in range(CAP):
                tag = tags[k, side * CAP + c : side * CAP + c + 1, :]
                value = rows[0, g].astype(F32)
                for f in range(1, nf):
                    value = jnp.where(tag == float(f), rows[f, g].astype(F32), value)
                out[k, side, g, c] = value.astype(BF16)

        def body(k):
            pick(tag_recv, k, back)
            ret_copy(k, side, g).start()
        loop(1, half, body)
        pick(tag_send, 0, ret)

    for g in range(2):
        def finish(f, g=g):
            far_copy(f, g).wait()
            value = part_sum[f, g] - far_recv[f, g].astype(F32)
            res_ref[f, g] = value
            res_bf[f, g] = value.astype(BF16)
            mid_copy(f, g).start()
        loop(0, nf, finish)
        give_back(NEAR, g, res_bf)
    for g in range(2):
        def wait_mid(f, g=g):
            mid_copy(f, g).wait()
        loop(0, nf, wait_mid)
        give_back(FAR, g, back_recv)

    def wait_ret(k):
        for side in range(2):
            for g in range(2):
                ret_copy(k, side, g).wait()
    loop(1, half, wait_ret)

    scale = 1.0 / ns

    def make_gradient(t):
        row = rows_ref[t]
        position = jnp.int32(0)
        for other in range(slots):
            same = jnp.logical_and(rows_ref[other] == row, other < t)
            position = jnp.where(same, jnp.int32(1), position)
        side = jnp.where(jnp.logical_and(row >= base, row < base + half), NEAR, FAR)
        k = lax.rem(row + n - local, half)
        left = jnp.concatenate([ret[k, side, 0, position], ret[k, side, 1, position]], axis=1)
        out = lax.dot_general(left, src[freqs_ref[t]], (((1,), (1,)), ((), ())),
                              preferred_element_type=F32)
        out = (-out * scale).astype(BF16)
        grad_ref[t, 0] = out[:, :nb]
        grad_ref[t, 1] = out[:, nb:]
    loop(0, slots, make_gradient)


def per_device(data, wavelet, panel_block, tiles, cover_rows, cover_freqs):
    nf, _, nb, ns = data.shape
    n = lax.axis_size("tiles")
    half = n // 2
    dma = pltpu.SemaphoreType.DMA
    smem = pl.BlockSpec(memory_space=pltpu.SMEM)
    vmem = pl.BlockSpec(memory_space=pltpu.VMEM)
    parcels = pltpu.VMEM((half, 2, 2, CAP, nb, ns), BF16)
    panel = pltpu.VMEM((nf, 2, nb, ns), BF16)
    return pl.pallas_call(
        functools.partial(kernel, n),
        out_shape=(
            jax.ShapeDtypeStruct(data.shape, F32),
            jax.ShapeDtypeStruct(tiles.shape, BF16),
        ),
        in_specs=[smem] * 4 + [vmem] * 2,
        out_specs=(vmem, vmem),
        scratch_shapes=[
            pltpu.VMEM((nf, 2 * nb, 2 * ns), BF16),
            pltpu.VMEM((half, 8, ns), F32),
            pltpu.VMEM((half, 8, ns), F32),
            parcels,
            parcels,
            pltpu.VMEM((nf, 2, nb, ns), F32),
            panel,
            panel,
            panel,
            panel,
            parcels,
            parcels,
            dma((half,)), dma((half,)),
            dma((half, 2, 2)), dma((half, 2, 2)),
            dma((nf, 2)), dma((nf, 2)),
            dma((nf, 2)), dma((nf, 2)),
            dma((half, 2, 2)), dma((half, 2, 2)),
        ],
        compiler_params=pltpu.CompilerParams(
            collective_id=0, has_side_effects=True, vmem_limit_bytes=60 * 1024 * 1024
        ),
    )(wavelet, panel_block, cover_rows, cover_freqs, data, tiles)


def solution(mesh):
    in_specs = (
        P("windows", None, "tiles", None),
        P(),
        P(),
        P(("windows", "tiles"), None, None, None),
        P(("windows", "tiles")),
        P(("windows", "tiles")),
    )
    out_specs = (P("windows", None, "tiles", None), P(("windows", "tiles"), None, None, None))
    return jax.shard_map(
        per_device, mesh=mesh, in_specs=in_specs, out_specs=out_specs, check_vma=False
    )
```

```python
import functools

import jax
import jax.numpy as jnp
from jax import lax
from jax.experimental import pallas as pl
from jax.experimental.pallas import tpu as pltpu
from jax.sharding import PartitionSpec as P

CAP = 2
GROUPS = 4
UP, DOWN = 0, 1
F32, BF16 = jnp.float32, jnp.bfloat16


def kernel(
    n, wav_ref, panel_ref, rows_ref, freqs_ref, data_ref, tiles_ref, res_ref, grad_ref,
    src, found, tag_send, tag_recv, send, recv, hop_send, hop_recv, rows_bf, back, ret,
    s_tag, r_tag, s_fwd, r_fwd, s_hop, r_hop, s_row, r_row, s_ret, r_ret,
):
    nf, _, nb, ns = data_ref.shape
    slots = tiles_ref.shape[0]
    width = n // GROUPS
    last = GROUPS - 1
    me = lax.axis_index("tiles")
    z = me // width
    local = lax.rem(me, width)

    def ahead(k):
        return z * width + lax.rem(local + k, width)

    def behind(k):
        return z * width + lax.rem(local + width - k, width)

    def remote(src_ref, dst_ref, s_sem, r_sem, device):
        return pltpu.make_async_remote_copy(
            src_ref=src_ref, dst_ref=dst_ref, send_sem=s_sem, recv_sem=r_sem,
            device_id={"tiles": device}, device_id_type=pl.DeviceIdType.MESH,
        )

    def tag_copy(k):
        return remote(tag_send.at[k], tag_recv.at[k], s_tag.at[k], r_tag.at[k], ahead(k))

    def fwd_copy(k, r, g):
        return remote(send.at[k, r, g], recv.at[k, r, g],
                      s_fwd.at[k, r, g], r_fwd.at[k, r, g], ahead(k))

    def next_device(way):
        return me + width if way == UP else me - width

    def hop_copy(way, r, f, g):
        return remote(hop_send.at[r, g, f], hop_recv.at[way, r, g, f],
                      s_hop.at[r, g, f], r_hop.at[way, r, g, f], next_device(way))

    def row_copy(way, r, f, g):
        return remote(rows_bf.at[r, g, f], rows_bf.at[r, g, f],
                      s_row.at[way, r, g, f], r_row.at[r, g, f], next_device(way))

    def ret_copy(k, r, g):
        return remote(back.at[k, r, g], ret.at[k, r, g],
                      s_ret.at[k, r, g], r_ret.at[k, r, g], behind(k))

    def loop(lo, hi, body):
        def step(i, carry):
            body(i)
            return carry
        lax.fori_loop(lo, hi, step, 0)

    barrier = pltpu.get_barrier_semaphore()

    def greet(device):
        pl.semaphore_signal(barrier, inc=1, device_id={"tiles": device},
                            device_id_type=pl.DeviceIdType.MESH)
    loop(1, width, lambda k: greet(ahead(k)))

    @pl.when(z < last)
    def _():
        greet(me + width)

    @pl.when(z > 0)
    def _():
        greet(me - width)

    eye = lax.broadcasted_iota(jnp.int32, (nb, ns), 0) == lax.broadcasted_iota(jnp.int32, (nb, ns), 1)
    at_panel = jnp.where(me == panel_ref[0], 1.0, 0.0).astype(F32)

    def make_source(f):
        re = jnp.where(eye, at_panel * wav_ref[f, 0], 0.0) - data_ref[f, 0].astype(F32)
        im = jnp.where(eye, at_panel * wav_ref[f, 1], 0.0) - data_ref[f, 1].astype(F32)
        re, im = re.astype(BF16), im.astype(BF16)
        src[f, :nb, :ns] = re
        src[f, :nb, ns:] = im
        src[f, nb:, :ns] = -im
        src[f, nb:, ns:] = re
    loop(0, nf, make_source)

    def find(k):
        for r in range(GROUPS):
            row = r * width + lax.rem(local + k, width)
            first = jnp.int32(-1)
            second = jnp.int32(-1)
            for t in reversed(range(slots)):
                hit = rows_ref[t] == row
                second = jnp.where(hit, first, second)
                first = jnp.where(hit, jnp.int32(t), first)
            for c, t in enumerate((first, second)):
                found[(k * GROUPS + r) * CAP + c] = jnp.maximum(t, 0)
                tag = jnp.where(t >= 0, freqs_ref[jnp.maximum(t, 0)], -1).astype(F32)
                tag_send[k, r * CAP + c : r * CAP + c + 1, :] = jnp.full((1, ns), tag, F32)
    loop(0, width, find)

    def make_parts(k, r):
        for c in range(CAP):
            at = found[(k * GROUPS + r) * CAP + c]
            left = jnp.concatenate([tiles_ref[at, 0], tiles_ref[at, 1]], axis=1)
            part = jnp.dot(left, src[freqs_ref[at]], preferred_element_type=F32).astype(BF16)
            send[k, r, 0, c] = part[:, :ns]
            send[k, r, 1, c] = part[:, ns:]

    order = []
    for i in range(GROUPS):
        options = ORDERS[i]
        value = jnp.int32(options[0])
        for at in range(1, GROUPS):
            value = jnp.where(z == at, jnp.int32(options[at]), value)
        order.append(value)

    pl.semaphore_wait(barrier, width - 1 + jnp.where(z > 0, 1, 0) + jnp.where(z < last, 1, 0))
    loop(1, width, lambda k: tag_copy(k).start())

    for r in order:
        def send_parts(k, r=r):
            make_parts(k, r)
            fwd_copy(k, r, 0).start()
            fwd_copy(k, r, 1).start()
        loop(1, width, send_parts)
        make_parts(0, r)
    loop(1, width, lambda k: tag_copy(k).wait())

    def gathered(r, f, g):
        want = f.astype(F32)

        def add(tags, parts, k, acc):
            for c in range(CAP):
                tag = tags[k, pl.ds(r * CAP + c, 1), :]
                acc = acc + jnp.where(tag == want, parts[k, r, g, c].astype(F32), 0.0)
            return acc
        acc = add(tag_send, send, 0, jnp.zeros((nb, ns), F32))
        return lax.fori_loop(1, width, functools.partial(add, tag_recv, recv), acc,
                             unroll=width <= 4)

    for r in order[:-1]:
        for g in range(2):
            loop(1, width, lambda k: fwd_copy(k, r, g).wait_recv())
            for way in (UP, DOWN):
                @pl.when(r > z if way == UP else r < z)
                def _(r=r, g=g, way=way):
                    inner = z > 0 if way == UP else z < last

                    @pl.when(inner)
                    def _():
                        def add_on(f):
                            acc = gathered(r, f, g)
                            hop_copy(way, r, f, g).wait_recv()
                            acc = acc + hop_recv[way, r, g, f].astype(F32)
                            hop_send[r, g, f] = acc.astype(BF16)
                            hop_copy(way, r, f, g).start()
                        loop(0, nf, add_on)

                    @pl.when(jnp.logical_not(inner))
                    def _():
                        def begin(f):
                            hop_send[r, g, f] = gathered(r, f, g).astype(BF16)
                            hop_copy(way, r, f, g).start()
                        loop(0, nf, begin)

    for g in range(2):
        loop(1, width, lambda k: fwd_copy(k, z, g).wait_recv())

        def subtract(f, g=g):
            res_ref[f, g] = data_ref[f, g].astype(F32) - gathered(z, f, g)
        loop(0, nf, subtract)

    def give_back(r, g):
        def pick(tags, k, out):
            for c in range(CAP):
                tag = tags[k, pl.ds(r * CAP + c, 1), :]
                value = rows_bf[r, g, 0].astype(F32)
                for f in range(1, nf):
                    value = jnp.where(tag == float(f), rows_bf[r, g, f].astype(F32), value)
                out[k, r, g, c] = value.astype(BF16)

        def body(k):
            pick(tag_recv, k, back)
            ret_copy(k, r, g).start()
        loop(1, width, body)
        pick(tag_send, 0, ret)

    for g in range(2):
        def finish(f, g=g):
            @pl.when(z > 0)
            def _():
                hop_copy(UP, z, f, g).wait_recv()
                res_ref[f, g] = res_ref[f, g] - hop_recv[UP, z, g, f].astype(F32)

            @pl.when(z < last)
            def _():
                hop_copy(DOWN, z, f, g).wait_recv()
                res_ref[f, g] = res_ref[f, g] - hop_recv[DOWN, z, g, f].astype(F32)
            rows_bf[z, g, f] = res_ref[f, g].astype(BF16)

            @pl.when(z < last)
            def _():
                row_copy(UP, z, f, g).start()

            @pl.when(z > 0)
            def _():
                row_copy(DOWN, z, f, g).start()
        loop(0, nf, finish)

    arrivals = []
    for i in range(GROUPS - 1):
        options = ARRIVALS[i]
        value = jnp.int32(options[0])
        for at in range(1, GROUPS):
            value = jnp.where(z == at, jnp.int32(options[at]), value)
        arrivals.append(value)

    for g in range(2):
        give_back(z, g)
    for r in arrivals:
        for g in range(2):
            def pass_on(f, r=r, g=g):
                row_copy(UP, r, f, g).wait_recv()

                @pl.when(jnp.logical_and(r < z, z < last))
                def _():
                    row_copy(UP, r, f, g).start()

                @pl.when(jnp.logical_and(r > z, z > 0))
                def _():
                    row_copy(DOWN, r, f, g).start()
            loop(0, nf, pass_on)
            give_back(r, g)

    for r in range(GROUPS):
        for g in range(2):
            loop(1, width, lambda k: ret_copy(k, r, g).wait_recv())

    scale = 1.0 / ns

    def make_gradient(t):
        row = rows_ref[t]
        position = jnp.int32(0)
        for other in range(slots):
            same = jnp.logical_and(rows_ref[other] == row, other < t)
            position = jnp.where(same, jnp.int32(1), position)
        r = row // width
        k = lax.rem(row + width - local, width)
        left = jnp.concatenate([ret[k, r, 0, position], ret[k, r, 1, position]], axis=1)
        out = lax.dot_general(left, src[freqs_ref[t]], (((1,), (1,)), ((), ())),
                              preferred_element_type=F32)
        out = (-out * scale).astype(BF16)
        grad_ref[t, 0] = out[:, :nb]
        grad_ref[t, 1] = out[:, nb:]
    loop(0, slots, make_gradient)

    for r in range(GROUPS):
        for g in range(2):
            def sent(k, r=r, g=g):
                fwd_copy(k, r, g).wait_send()
                ret_copy(k, r, g).wait_send()
            loop(1, width, sent)

            def hopped(f, r=r, g=g):
                @pl.when(r != z)
                def _():
                    hop_copy(UP, r, f, g).wait_send()

                @pl.when(jnp.logical_and(r <= z, z < last))
                def _():
                    row_copy(UP, r, f, g).wait_send()

                @pl.when(jnp.logical_and(r >= z, z > 0))
                def _():
                    row_copy(DOWN, r, f, g).wait_send()
            loop(0, nf, hopped)


ORDERS = ((3, 3, 0, 0), (2, 0, 3, 1), (1, 2, 1, 2), (0, 1, 2, 3))
ARRIVALS = ((1, 0, 3, 2), (2, 2, 1, 1), (3, 3, 0, 0))


def per_device(data, wavelet, panel_block, tiles, cover_rows, cover_freqs):
    nf, _, nb, ns = data.shape
    n = lax.axis_size("tiles")
    width = n // GROUPS
    dma = pltpu.SemaphoreType.DMA
    smem = pl.BlockSpec(memory_space=pltpu.SMEM)
    vmem = pl.BlockSpec(memory_space=pltpu.VMEM)
    parcels = pltpu.VMEM((width, GROUPS, 2, CAP, nb, ns), BF16)
    tags = pltpu.VMEM((width, GROUPS * CAP, ns), F32)
    panels = (GROUPS, 2, nf)
    return pl.pallas_call(
        functools.partial(kernel, n),
        out_shape=(
            jax.ShapeDtypeStruct(data.shape, F32),
            jax.ShapeDtypeStruct(tiles.shape, BF16),
        ),
        in_specs=[smem] * 4 + [vmem] * 2,
        out_specs=(vmem, vmem),
        scratch_shapes=[
            pltpu.VMEM((nf, 2 * nb, 2 * ns), BF16),
            pltpu.SMEM((n * CAP,), jnp.int32),
            tags,
            tags,
            parcels,
            parcels,
            pltpu.VMEM(panels + (nb, ns), BF16),
            pltpu.VMEM((2,) + panels + (nb, ns), BF16),
            pltpu.VMEM(panels + (nb, ns), BF16),
            parcels,
            parcels,
            dma((width,)), dma((width,)),
            dma((width, GROUPS, 2)), dma((width, GROUPS, 2)),
            dma(panels), dma((2,) + panels),
            dma((2,) + panels), dma(panels),
            dma((width, GROUPS, 2)), dma((width, GROUPS, 2)),
        ],
        compiler_params=pltpu.CompilerParams(
            collective_id=0, has_side_effects=True, vmem_limit_bytes=60 * 1024 * 1024
        ),
    )(wavelet, panel_block, cover_rows, cover_freqs, data, tiles)


def solution(mesh):
    in_specs = (
        P("windows", None, "tiles", None),
        P(),
        P(),
        P(("windows", "tiles"), None, None, None),
        P(("windows", "tiles")),
        P(("windows", "tiles")),
    )
    out_specs = (P("windows", None, "tiles", None), P(("windows", "tiles"), None, None, None))
    return jax.shard_map(
        per_device, mesh=mesh, in_specs=in_specs, out_specs=out_specs, check_vma=False
    )
```

```python
import functools

import jax
import jax.numpy as jnp
from jax import lax
from jax.experimental import pallas as pl
from jax.experimental.pallas import tpu as pltpu
from jax.sharding import PartitionSpec as P

CAP = 2
GROUPS = 4
UP, DOWN = 0, 1
LAG = 4
F32, BF16 = jnp.float32, jnp.bfloat16


def kernel(
    n, wav_ref, panel_ref, rows_ref, freqs_ref, data_ref, tiles_ref, res_ref, grad_ref,
    src, found, tag_send, tag_recv, send, recv, hop_send, hop_recv, rows_bf, back, ret,
    s_tag, r_tag, s_fwd, r_fwd, s_hop, r_hop, s_row, r_row, s_ret, r_ret,
):
    nf, _, nb, ns = data_ref.shape
    slots = tiles_ref.shape[0]
    width = n // GROUPS
    last = GROUPS - 1
    me = lax.axis_index("tiles")
    z = me // width
    local = lax.rem(me, width)

    def ahead(k):
        return z * width + lax.rem(local + k, width)

    def behind(k):
        return z * width + lax.rem(local + width - k, width)

    def remote(src_ref, dst_ref, s_sem, r_sem, device):
        return pltpu.make_async_remote_copy(
            src_ref=src_ref, dst_ref=dst_ref, send_sem=s_sem, recv_sem=r_sem,
            device_id={"tiles": device}, device_id_type=pl.DeviceIdType.MESH,
        )

    def tag_copy(k):
        return remote(tag_send.at[k], tag_recv.at[k], s_tag.at[k], r_tag.at[k], ahead(k))

    def fwd_copy(k, r, g):
        return remote(send.at[k, r, g], recv.at[k, r, g],
                      s_fwd.at[k, r, g], r_fwd.at[k, r, g], ahead(k))

    def next_device(way):
        return me + width * (1 - 2 * way)

    def hop_copy(way, r, f, g):
        return remote(hop_send.at[r, g, f], hop_recv.at[way, r, g, f],
                      s_hop.at[r, g, f], r_hop.at[way, r, g, f], next_device(way))

    def row_copy(way, r, f, g):
        return remote(rows_bf.at[r, g, f], rows_bf.at[r, g, f],
                      s_row.at[way, r, g, f], r_row.at[r, g, f], next_device(way))

    def ret_copy(k, r, g):
        return remote(back.at[k, r, g], ret.at[k, r, g],
                      s_ret.at[k, r, g], r_ret.at[k, r, g], behind(k))

    def loop(lo, hi, body):
        def step(i, carry):
            body(i)
            return carry
        lax.fori_loop(lo, hi, step, 0)

    barrier = pltpu.get_barrier_semaphore()

    def greet(device):
        pl.semaphore_signal(barrier, inc=1, device_id={"tiles": device},
                            device_id_type=pl.DeviceIdType.MESH)
    loop(1, width, lambda k: greet(ahead(k)))

    @pl.when(z < last)
    def _():
        greet(me + width)

    @pl.when(z > 0)
    def _():
        greet(me - width)

    eye = lax.broadcasted_iota(jnp.int32, (nb, ns), 0) == lax.broadcasted_iota(jnp.int32, (nb, ns), 1)
    at_panel = jnp.where(me == panel_ref[0], 1.0, 0.0).astype(F32)

    def make_source(f):
        re = jnp.where(eye, at_panel * wav_ref[f, 0], 0.0) - data_ref[f, 0].astype(F32)
        im = jnp.where(eye, at_panel * wav_ref[f, 1], 0.0) - data_ref[f, 1].astype(F32)
        re, im = re.astype(BF16), im.astype(BF16)
        src[f, :nb, :ns] = re
        src[f, :nb, ns:] = im
        src[f, nb:, :ns] = -im
        src[f, nb:, ns:] = re
    loop(0, nf, make_source)

    def find(k):
        for r in range(GROUPS):
            row = r * width + lax.rem(local + k, width)
            first = jnp.int32(-1)
            second = jnp.int32(-1)
            for t in reversed(range(slots)):
                hit = rows_ref[t] == row
                second = jnp.where(hit, first, second)
                first = jnp.where(hit, jnp.int32(t), first)
            for c, t in enumerate((first, second)):
                found[(k * GROUPS + r) * CAP + c] = jnp.maximum(t, 0)
                tag = jnp.where(t >= 0, freqs_ref[jnp.maximum(t, 0)], -1).astype(F32)
                tag_send[k, r * CAP + c : r * CAP + c + 1, :] = jnp.full((1, ns), tag, F32)
    loop(0, width, find)

    def make_parts(k, r):
        for c in range(CAP):
            at = found[(k * GROUPS + r) * CAP + c]
            left = jnp.concatenate([tiles_ref[at, 0], tiles_ref[at, 1]], axis=1)
            part = jnp.dot(left, src[freqs_ref[at]], preferred_element_type=F32).astype(BF16)
            send[k, r, 0, c] = part[:, :ns]
            send[k, r, 1, c] = part[:, ns:]

    low = z < GROUPS // 2
    inward = jnp.where(low, UP, DOWN)
    outward = 1 - inward
    outer = jnp.logical_or(z == 0, z == last)

    def group(c):
        return jnp.where(low, c, last - c)

    pl.semaphore_wait(barrier, width - 1 + jnp.where(z > 0, 1, 0) + jnp.where(z < last, 1, 0))
    loop(1, width, lambda k: tag_copy(k).start())

    for r in (group(3), group(0), group(2), group(1)):
        def send_parts(k, r=r):
            make_parts(k, r)
            fwd_copy(k, r, 0).start()
            fwd_copy(k, r, 1).start()
        loop(1, width, send_parts)
        make_parts(0, r)
    loop(1, width, lambda k: tag_copy(k).wait())

    def gathered(r, f, g):
        want = f.astype(F32)

        def add(tags, parts, k, acc):
            for c in range(CAP):
                tag = tags[k, pl.ds(r * CAP + c, 1), :]
                acc = acc + jnp.where(tag == want, parts[k, r, g, c].astype(F32), 0.0)
            return acc
        acc = add(tag_send, send, 0, jnp.zeros((nb, ns), F32))
        return lax.fori_loop(1, width, functools.partial(add, tag_recv, recv), acc,
                             unroll=width <= 4)

    pieces = 2 * nf

    def wait_plane(r, g):
        loop(1, width, lambda k: fwd_copy(k, r, g).wait_recv())

    def arrived(way, r, f, g):
        hop_copy(way, r, f, g).wait_recv()
        return hop_recv[way, r, g, f].astype(F32)

    def begin(r, f, g):
        hop_send[r, g, f] = gathered(r, f, g).astype(BF16)
        hop_copy(inward, r, f, g).start()

    def add_on(way, r, f, g):
        acc = gathered(r, f, g) + arrived(way, r, f, g)
        hop_send[r, g, f] = acc.astype(BF16)
        hop_copy(way, r, f, g).start()

    def pass_on(way, r, f, g):
        row_copy(way, r, f, g).wait_recv()
        row_copy(way, r, f, g).start()

    def wait_row(r, g):
        loop(0, nf, lambda f: row_copy(UP, r, f, g).wait_recv())

    def give_back(r, g):
        def pick(tags, k, out):
            for c in range(CAP):
                tag = tags[k, pl.ds(r * CAP + c, 1), :]
                value = rows_bf[r, g, 0].astype(F32)
                for f in range(1, nf):
                    value = jnp.where(tag == float(f), rows_bf[r, g, f].astype(F32), value)
                out[k, r, g, c] = value.astype(BF16)

        def body(k):
            pick(tag_recv, k, back)
            ret_copy(k, r, g).start()
        loop(1, width, body)
        pick(tag_send, 0, ret)

    @pl.when(outer)
    def _():
        for g in range(2):
            wait_plane(group(3), g)
            loop(0, nf, lambda f: begin(group(3), f, g))
        for g in range(2):
            wait_plane(z, g)

            def finish(f, g=g):
                value = data_ref[f, g].astype(F32) - gathered(z, f, g)
                value = value - arrived(outward, z, f, g)
                res_ref[f, g] = value
                rows_bf[z, g, f] = value.astype(BF16)
                row_copy(inward, z, f, g).start()
            loop(0, nf, finish)
        for g in range(2):
            wait_plane(group(2), g)
            wait_plane(group(1), g)

            def begin_two(f, g=g):
                begin(group(2), f, g)
                begin(group(1), f, g)
            loop(0, nf, begin_two)
        give_back(z, 0)
        give_back(z, 1)
        for g in range(2):
            wait_row(group(3), g)
            give_back(group(3), g)
        for g in range(2):
            for c in (1, 2):
                wait_row(group(c), g)
                give_back(group(c), g)

    @pl.when(jnp.logical_not(outer))
    def _():
        def end_row(f, g):
            value = data_ref[f, g].astype(F32) - gathered(z, f, g)
            value = value - arrived(UP, z, f, g) - arrived(DOWN, z, f, g)
            res_ref[f, g] = value
            rows_bf[z, g, f] = value.astype(BF16)
            row_copy(inward, z, f, g).start()
            row_copy(outward, z, f, g).start()

        tasks = (
            (0, lambda f, g: add_on(inward, group(3), f, g)),
            (LAG, lambda f, g: add_on(outward, group(0), f, g)),
            (pieces, lambda f, g: pass_on(inward, group(0), f, g)),
            (pieces + LAG, lambda f, g: pass_on(outward, group(3), f, g)),
            (2 * pieces, lambda f, g: add_on(inward, group(2), f, g)),
            (2 * pieces + LAG, end_row),
            (2 * pieces + 2 * LAG, lambda f, g: pass_on(outward, group(2), f, g)),
        )
        handed = (
            (2 * pieces + 2, 0, 0), (2 * pieces + 4, 0, 1),
            (2 * pieces + LAG + 1, 3, 0), (2 * pieces + LAG + 3, 3, 1),
            (2 * pieces + LAG + nf, 1, 0), (2 * pieces + 2 * LAG + nf, 2, 0),
            (3 * pieces + LAG, 1, 1),
        )
        for g in range(2):
            wait_plane(group(3), g)
            wait_plane(group(0), g)

        def step(i):
            @pl.when(i == 2 * pieces)
            def _():
                for g in range(2):
                    wait_plane(group(2), g)
                    wait_plane(z, g)
            for first, task in tasks:
                @pl.when(jnp.logical_and(i >= first, i < first + pieces))
                def _(first=first, task=task):
                    p = i - first
                    g = jnp.where(p >= nf, 1, 0)
                    task(p - g * nf, g)
            for at, c, g in handed:
                @pl.when(i == at)
                def _(c=c, g=g):
                    give_back(group(c), g)
        loop(0, 3 * pieces + 2 * LAG, step)
        give_back(group(2), 1)

    for r in range(GROUPS):
        for g in range(2):
            loop(1, width, lambda k: ret_copy(k, r, g).wait_recv())

    scale = 1.0 / ns

    def make_gradient(t):
        row = rows_ref[t]
        position = jnp.int32(0)
        for other in range(slots):
            same = jnp.logical_and(rows_ref[other] == row, other < t)
            position = jnp.where(same, jnp.int32(1), position)
        r = row // width
        k = lax.rem(row + width - local, width)
        left = jnp.concatenate([ret[k, r, 0, position], ret[k, r, 1, position]], axis=1)
        out = lax.dot_general(left, src[freqs_ref[t]], (((1,), (1,)), ((), ())),
                              preferred_element_type=F32)
        out = (-out * scale).astype(BF16)
        grad_ref[t, 0] = out[:, :nb]
        grad_ref[t, 1] = out[:, nb:]
    loop(0, slots, make_gradient)

    for r in range(GROUPS):
        for g in range(2):
            def sent(k, r=r, g=g):
                fwd_copy(k, r, g).wait_send()
                ret_copy(k, r, g).wait_send()
            loop(1, width, sent)

            def hopped(f, r=r, g=g):
                @pl.when(r != z)
                def _():
                    hop_copy(UP, r, f, g).wait_send()

                @pl.when(jnp.logical_and(r <= z, z < last))
                def _():
                    row_copy(UP, r, f, g).wait_send()

                @pl.when(jnp.logical_and(r >= z, z > 0))
                def _():
                    row_copy(DOWN, r, f, g).wait_send()
            loop(0, nf, hopped)


def per_device(data, wavelet, panel_block, tiles, cover_rows, cover_freqs):
    nf, _, nb, ns = data.shape
    n = lax.axis_size("tiles")
    width = n // GROUPS
    dma = pltpu.SemaphoreType.DMA
    smem = pl.BlockSpec(memory_space=pltpu.SMEM)
    vmem = pl.BlockSpec(memory_space=pltpu.VMEM)
    parcels = pltpu.VMEM((width, GROUPS, 2, CAP, nb, ns), BF16)
    tags = pltpu.VMEM((width, GROUPS * CAP, ns), F32)
    panels = (GROUPS, 2, nf)
    return pl.pallas_call(
        functools.partial(kernel, n),
        out_shape=(
            jax.ShapeDtypeStruct(data.shape, F32),
            jax.ShapeDtypeStruct(tiles.shape, BF16),
        ),
        in_specs=[smem] * 4 + [vmem] * 2,
        out_specs=(vmem, vmem),
        scratch_shapes=[
            pltpu.VMEM((nf, 2 * nb, 2 * ns), BF16),
            pltpu.SMEM((n * CAP,), jnp.int32),
            tags,
            tags,
            parcels,
            parcels,
            pltpu.VMEM(panels + (nb, ns), BF16),
            pltpu.VMEM((2,) + panels + (nb, ns), BF16),
            pltpu.VMEM(panels + (nb, ns), BF16),
            parcels,
            parcels,
            dma((width,)), dma((width,)),
            dma((width, GROUPS, 2)), dma((width, GROUPS, 2)),
            dma(panels), dma((2,) + panels),
            dma((2,) + panels), dma(panels),
            dma((width, GROUPS, 2)), dma((width, GROUPS, 2)),
        ],
        compiler_params=pltpu.CompilerParams(
            collective_id=0, has_side_effects=True, vmem_limit_bytes=60 * 1024 * 1024
        ),
    )(wavelet, panel_block, cover_rows, cover_freqs, data, tiles)


def solution(mesh):
    in_specs = (
        P("windows", None, "tiles", None),
        P(),
        P(),
        P(("windows", "tiles"), None, None, None),
        P(("windows", "tiles")),
        P(("windows", "tiles")),
    )
    out_specs = (P("windows", None, "tiles", None), P(("windows", "tiles"), None, None, None))
    return jax.shard_map(
        per_device, mesh=mesh, in_specs=in_specs, out_specs=out_specs, check_vma=False
    )
```

```python
import functools

import jax
import jax.numpy as jnp
from jax import lax
from jax.experimental import pallas as pl
from jax.experimental.pallas import tpu as pltpu
from jax.sharding import PartitionSpec as P

CAP = 2
GROUPS = 4
UP, DOWN = 0, 1
LAG = 4
F32, BF16 = jnp.float32, jnp.bfloat16


def kernel(
    n, wav_ref, panel_ref, rows_ref, freqs_ref, data_ref, tiles_ref, res_ref, grad_ref,
    src, found, tag_send, tag_recv, send, recv, hop_send, hop_recv, rows_bf, back, ret,
    s_tag, r_tag, s_fwd, r_fwd, s_hop, r_hop, s_row, r_row, s_ret, r_ret,
):
    nf, _, nb, ns = data_ref.shape
    slots = tiles_ref.shape[0]
    width = n // GROUPS
    last = GROUPS - 1
    me = lax.axis_index("tiles")
    z = me // width
    local = lax.rem(me, width)

    def ahead(k):
        return z * width + lax.rem(local + k, width)

    def behind(k):
        return z * width + lax.rem(local + width - k, width)

    def remote(src_ref, dst_ref, s_sem, r_sem, device):
        return pltpu.make_async_remote_copy(
            src_ref=src_ref, dst_ref=dst_ref, send_sem=s_sem, recv_sem=r_sem,
            device_id={"tiles": device}, device_id_type=pl.DeviceIdType.MESH,
        )

    def tag_copy(k):
        return remote(tag_send.at[k], tag_recv.at[k], s_tag.at[k], r_tag.at[k], ahead(k))

    def fwd_copy(k, r, g):
        return remote(send.at[k, r, g], recv.at[k, r, g],
                      s_fwd.at[k, r, g], r_fwd.at[k, r, g], ahead(k))

    def next_device(way):
        return me + width * (1 - 2 * way)

    def hop_copy(way, r, f, g):
        return remote(hop_send.at[r, g, f], hop_recv.at[way, r, g, f],
                      s_hop.at[r, g, f], r_hop.at[way, r, g, f], next_device(way))

    def row_copy(way, r, f, g):
        return remote(rows_bf.at[r, g, f], rows_bf.at[r, g, f],
                      s_row.at[way, r, g, f], r_row.at[r, g, f], next_device(way))

    def ret_copy(k, r, g):
        return remote(back.at[k, r, g], ret.at[k, r, g],
                      s_ret.at[k, r, g], r_ret.at[k, r, g], behind(k))

    def loop(lo, hi, body):
        def step(i, carry):
            body(i)
            return carry
        lax.fori_loop(lo, hi, step, 0)

    barrier = pltpu.get_barrier_semaphore()

    def greet(device):
        pl.semaphore_signal(barrier, inc=1, device_id={"tiles": device},
                            device_id_type=pl.DeviceIdType.MESH)
    loop(1, width, lambda k: greet(ahead(k)))

    @pl.when(z < last)
    def _():
        greet(me + width)

    @pl.when(z > 0)
    def _():
        greet(me - width)

    eye = lax.broadcasted_iota(jnp.int32, (nb, ns), 0) == lax.broadcasted_iota(jnp.int32, (nb, ns), 1)
    at_panel = jnp.where(me == panel_ref[0], 1.0, 0.0).astype(F32)

    def make_source(f):
        re = jnp.where(eye, at_panel * wav_ref[f, 0], 0.0) - data_ref[f, 0].astype(F32)
        im = jnp.where(eye, at_panel * wav_ref[f, 1], 0.0) - data_ref[f, 1].astype(F32)
        re, im = re.astype(BF16), im.astype(BF16)
        src[f, :nb, :ns] = re
        src[f, :nb, ns:] = im
        src[f, nb:, :ns] = -im
        src[f, nb:, ns:] = re
    loop(0, nf, make_source)

    def find(k):
        for r in range(GROUPS):
            row = r * width + lax.rem(local + k, width)
            first = jnp.int32(-1)
            second = jnp.int32(-1)
            for t in reversed(range(slots)):
                hit = rows_ref[t] == row
                second = jnp.where(hit, first, second)
                first = jnp.where(hit, jnp.int32(t), first)
            for c, t in enumerate((first, second)):
                found[(k * GROUPS + r) * CAP + c] = jnp.maximum(t, 0)
                tag = jnp.where(t >= 0, freqs_ref[jnp.maximum(t, 0)], -1).astype(F32)
                tag_send[k, r * CAP + c : r * CAP + c + 1, :] = jnp.full((1, ns), tag, F32)
    loop(0, width, find)

    def make_parts(k, r):
        for c in range(CAP):
            at = found[(k * GROUPS + r) * CAP + c]
            left = jnp.concatenate([tiles_ref[at, 0], tiles_ref[at, 1]], axis=1)
            part = jnp.dot(left, src[freqs_ref[at]], preferred_element_type=F32).astype(BF16)
            send[k, r, 0, c] = part[:, :ns]
            send[k, r, 1, c] = part[:, ns:]

    low = z < GROUPS // 2
    inward = jnp.where(low, UP, DOWN)
    outward = 1 - inward
    outer = jnp.logical_or(z == 0, z == last)

    def group(c):
        return jnp.where(low, c, last - c)

    pl.semaphore_wait(barrier, width - 1 + jnp.where(z > 0, 1, 0) + jnp.where(z < last, 1, 0))
    loop(1, width, lambda k: tag_copy(k).start())

    for r in (group(3), group(0), group(2), group(1)):
        def send_parts(k, r=r):
            make_parts(k, r)
            fwd_copy(k, r, 0).start()
            fwd_copy(k, r, 1).start()
        loop(1, width, send_parts)
        make_parts(0, r)
    loop(1, width, lambda k: tag_copy(k).wait())

    def gathered(r, f, g):
        want = f.astype(F32)

        def add(tags, parts, k, acc):
            for c in range(CAP):
                tag = tags[k, pl.ds(r * CAP + c, 1), :]
                acc = acc + jnp.where(tag == want, parts[k, r, g, c].astype(F32), 0.0)
            return acc
        acc = add(tag_send, send, 0, jnp.zeros((nb, ns), F32))
        return lax.fori_loop(1, width, functools.partial(add, tag_recv, recv), acc,
                             unroll=width <= 4)

    pieces = 2 * nf

    def wait_plane(r, g):
        loop(1, width, lambda k: fwd_copy(k, r, g).wait_recv())

    def arrived(way, r, f, g):
        hop_copy(way, r, f, g).wait_recv()
        return hop_recv[way, r, g, f].astype(F32)

    def begin(r, f, g):
        hop_send[r, g, f] = gathered(r, f, g).astype(BF16)
        hop_copy(inward, r, f, g).start()

    def add_on(way, r, f, g):
        acc = gathered(r, f, g) + arrived(way, r, f, g)
        hop_send[r, g, f] = acc.astype(BF16)
        hop_copy(way, r, f, g).start()

    def pass_on(way, r, f, g):
        row_copy(way, r, f, g).wait_recv()
        row_copy(way, r, f, g).start()

    def wait_row(r, g):
        loop(0, nf, lambda f: row_copy(UP, r, f, g).wait_recv())

    def give_back(r, g):
        def pick(tags, k, out):
            for c in range(CAP):
                tag = tags[k, pl.ds(r * CAP + c, 1), :]
                value = rows_bf[r, g, 0].astype(F32)
                for f in range(1, nf):
                    value = jnp.where(tag == float(f), rows_bf[r, g, f].astype(F32), value)
                out[k, r, g, c] = value.astype(BF16)

        def body(k):
            pick(tag_recv, k, back)
            ret_copy(k, r, g).start()
        loop(1, width, body)
        pick(tag_send, 0, ret)

    @pl.when(outer)
    def _():
        for g in range(2):
            wait_plane(group(3), g)
            loop(0, nf, lambda f: begin(group(3), f, g))
        for g in range(2):
            wait_plane(z, g)

            def finish(f, g=g):
                value = data_ref[f, g].astype(F32) - gathered(z, f, g)
                value = value - arrived(outward, z, f, g)
                res_ref[f, g] = value
                rows_bf[z, g, f] = value.astype(BF16)
                row_copy(inward, z, f, g).start()
            loop(0, nf, finish)
        for g in range(2):
            wait_plane(group(2), g)
            wait_plane(group(1), g)

            def begin_two(f, g=g):
                begin(group(2), f, g)
                begin(group(1), f, g)
            loop(0, nf, begin_two)
        give_back(z, 0)
        give_back(z, 1)
        for g in range(2):
            wait_row(group(3), g)
            give_back(group(3), g)
        for g in range(2):
            for c in (1, 2):
                wait_row(group(c), g)
                give_back(group(c), g)

    @pl.when(jnp.logical_not(outer))
    def _():
        def end_row(f, g):
            value = data_ref[f, g].astype(F32) - gathered(z, f, g)
            value = value - arrived(UP, z, f, g) - arrived(DOWN, z, f, g)
            res_ref[f, g] = value
            rows_bf[z, g, f] = value.astype(BF16)
            row_copy(inward, z, f, g).start()
            row_copy(outward, z, f, g).start()

        tasks = (
            (0, lambda f, g: add_on(inward, group(3), f, g)),
            (LAG, lambda f, g: add_on(outward, group(0), f, g)),
            (pieces, lambda f, g: pass_on(inward, group(0), f, g)),
            (pieces + LAG, lambda f, g: pass_on(outward, group(3), f, g)),
            (2 * pieces, lambda f, g: add_on(inward, group(2), f, g)),
            (2 * pieces + LAG, end_row),
            (2 * pieces + 2 * LAG, lambda f, g: pass_on(outward, group(2), f, g)),
        )
        handed = (
            (2 * pieces + 2, 0, 0), (2 * pieces + 4, 0, 1),
            (2 * pieces + LAG + 1, 3, 0), (2 * pieces + LAG + 3, 3, 1),
            (2 * pieces + LAG + nf, 1, 0), (2 * pieces + 2 * LAG + nf, 2, 0),
            (3 * pieces + LAG, 1, 1),
        )
        for g in range(2):
            wait_plane(group(3), g)
            wait_plane(group(0), g)

        def step(i):
            @pl.when(i == 2 * pieces)
            def _():
                for g in range(2):
                    wait_plane(group(2), g)
                    wait_plane(z, g)
            for first, task in tasks:
                @pl.when(jnp.logical_and(i >= first, i < first + pieces))
                def _(first=first, task=task):
                    p = i - first
                    g = jnp.where(p >= nf, 1, 0)
                    task(p - g * nf, g)
            for at, c, g in handed:
                @pl.when(i == at)
                def _(c=c, g=g):
                    give_back(group(c), g)
        loop(0, 3 * pieces + 2 * LAG, step)
        give_back(group(2), 1)

    for r in range(GROUPS):
        for g in range(2):
            loop(1, width, lambda k: ret_copy(k, r, g).wait_recv())

    scale = 1.0 / ns

    def make_gradient(t):
        row = rows_ref[t]
        position = jnp.int32(0)
        for other in range(slots):
            same = jnp.logical_and(rows_ref[other] == row, other < t)
            position = jnp.where(same, jnp.int32(1), position)
        r = row // width
        k = lax.rem(row + width - local, width)
        left = jnp.concatenate([ret[k, r, 0, position], ret[k, r, 1, position]], axis=1)
        out = lax.dot_general(left, src[freqs_ref[t]], (((1,), (1,)), ((), ())),
                              preferred_element_type=F32)
        out = (-out * scale).astype(BF16)
        grad_ref[t, 0] = out[:, :nb]
        grad_ref[t, 1] = out[:, nb:]
    def gradients(i, carry):
        make_gradient(i)
        return carry
    lax.fori_loop(0, slots, gradients, 0, unroll=4)

    for r in range(GROUPS):
        for g in range(2):
            def sent(k, r=r, g=g):
                fwd_copy(k, r, g).wait_send()
                ret_copy(k, r, g).wait_send()
            loop(1, width, sent)

            def hopped(f, r=r, g=g):
                @pl.when(r != z)
                def _():
                    hop_copy(UP, r, f, g).wait_send()

                @pl.when(jnp.logical_and(r <= z, z < last))
                def _():
                    row_copy(UP, r, f, g).wait_send()

                @pl.when(jnp.logical_and(r >= z, z > 0))
                def _():
                    row_copy(DOWN, r, f, g).wait_send()
            loop(0, nf, hopped)


def per_device(data, wavelet, panel_block, tiles, cover_rows, cover_freqs):
    nf, _, nb, ns = data.shape
    n = lax.axis_size("tiles")
    width = n // GROUPS
    dma = pltpu.SemaphoreType.DMA
    smem = pl.BlockSpec(memory_space=pltpu.SMEM)
    vmem = pl.BlockSpec(memory_space=pltpu.VMEM)
    parcels = pltpu.VMEM((width, GROUPS, 2, CAP, nb, ns), BF16)
    tags = pltpu.VMEM((width, GROUPS * CAP, ns), F32)
    panels = (GROUPS, 2, nf)
    return pl.pallas_call(
        functools.partial(kernel, n),
        out_shape=(
            jax.ShapeDtypeStruct(data.shape, F32),
            jax.ShapeDtypeStruct(tiles.shape, BF16),
        ),
        in_specs=[smem] * 4 + [vmem] * 2,
        out_specs=(vmem, vmem),
        scratch_shapes=[
            pltpu.VMEM((nf, 2 * nb, 2 * ns), BF16),
            pltpu.SMEM((n * CAP,), jnp.int32),
            tags,
            tags,
            parcels,
            parcels,
            pltpu.VMEM(panels + (nb, ns), BF16),
            pltpu.VMEM((2,) + panels + (nb, ns), BF16),
            pltpu.VMEM(panels + (nb, ns), BF16),
            parcels,
            parcels,
            dma((width,)), dma((width,)),
            dma((width, GROUPS, 2)), dma((width, GROUPS, 2)),
            dma(panels), dma((2,) + panels),
            dma((2,) + panels), dma(panels),
            dma((width, GROUPS, 2)), dma((width, GROUPS, 2)),
        ],
        compiler_params=pltpu.CompilerParams(
            collective_id=0, has_side_effects=True, vmem_limit_bytes=60 * 1024 * 1024
        ),
    )(wavelet, panel_block, cover_rows, cover_freqs, data, tiles)


def solution(mesh):
    in_specs = (
        P("windows", None, "tiles", None),
        P(),
        P(),
        P(("windows", "tiles"), None, None, None),
        P(("windows", "tiles")),
        P(("windows", "tiles")),
    )
    out_specs = (P("windows", None, "tiles", None), P(("windows", "tiles"), None, None, None))
    return jax.shard_map(
        per_device, mesh=mesh, in_specs=in_specs, out_specs=out_specs, check_vma=False
    )
```
